128 devices in a mesh: row: 16 (over y, z), col: 8 (over x, core).
Axes of the slice: x: 4, y: 4, z: 4, core: 2. Of those that a mesh axis runs over, the one named last changes fastest.
Arguments:
- data: float32 [64, 90112], P(None, 'row')
- blocks: float32 [36864, 128, 128], P(('row', 'col'))
- block_row: int32 [36864], P(('row', 'col')), may hold values from -1 to 703, as said below
- block_col: int32 [36864], P(('row', 'col')), may hold values from -1 to 703, as said below
Outputs:
- solution: float32 [64, 90112], P(None, 'col')
The draws below stay inside these ranges and needn't reach their ends.
Inputs may be any that keep to these rules, and one draw needn't show every extreme that they name: The slots come in runs of 288, run d for d = 0, 1, ...; in each run the live slots come first and the empty ones (-1 in block_row and block_col alike) after them; every run has a live slot and some run has no empty slot. A live slot of run d has block_row in (d // 8) * 44 to (d // 8 + 1) * 44 - 1. Empty in the same slots as block_row. A live slot of run d has block_col in (d % 8) * 88 to (d % 8 + 1) * 88 - 1.
All inputs are finite; a program needn't handle non-finite values.
Results may differ from the reference program's by a relative error of at most 0.0001.
Values sent between devices are 32-bit elements; how exact they have to be, the bound alone decides.
A program may use at most 128 MiB of HBM per device.

```python
import math
import jax
import jax.numpy as jnp
from jax import lax

EPOCHS = 64
BLOCK_EDGE = 128
DEV_SLOTS = 288
ROW_BLOCKS = 44
COL_BLOCKS = 88
ITERATIONS = 3
DATA_ROWS = 90112
UNKNOWNS = 90112
ALL_SLOTS = 36864
N_ROW = 16
N_COL = 8


def live_counts(key):
    device = jnp.arange(N_ROW * N_COL, dtype=jnp.int32)
    row_index = device // N_COL
    col_index = device % N_COL
    offset = jnp.abs((2 * row_index + 1) * N_COL - (2 * col_index + 1) * N_ROW) // (2 * N_COL)
    offset = jnp.minimum(offset, N_ROW - offset)
    base_count = DEV_SLOTS * 2 // (2 + offset)
    jitter = jax.random.randint(jax.random.fold_in(key, 7), (N_ROW * N_COL,), 0, DEV_SLOTS // 16 + 1)
    return jnp.where(offset == 0, DEV_SLOTS, jnp.maximum(base_count - jitter, 1))


def slot_alive(key):
    counts = live_counts(key)
    slot_number = jnp.arange(DEV_SLOTS, dtype=jnp.int32)
    return slot_number[None, :] < counts[:, None]


def draw_block_row(key, part):
    is_live = slot_alive(key)
    device = jnp.arange(N_ROW * N_COL, dtype=jnp.int32)
    first_row = device // N_COL * ROW_BLOCKS
    picked = jax.random.randint(jax.random.fold_in(key, 11), (N_ROW * N_COL, DEV_SLOTS), 0, ROW_BLOCKS)
    return jnp.where(is_live, first_row[:, None] + picked, -1).reshape(-1).astype(jnp.int32)


def draw_block_col(key, part):
    is_live = slot_alive(key)
    device = jnp.arange(N_ROW * N_COL, dtype=jnp.int32)
    first_col = device % N_COL * COL_BLOCKS
    picked = jax.random.randint(jax.random.fold_in(key, 13), (N_ROW * N_COL, DEV_SLOTS), 0, COL_BLOCKS)
    return jnp.where(is_live, first_col[:, None] + picked, -1).reshape(-1).astype(jnp.int32)


def draw_blocks(key, part):
    shape = (ALL_SLOTS, BLOCK_EDGE, BLOCK_EDGE)
    factor = 1.0 / math.sqrt(12.0 * BLOCK_EDGE)
    first_key = jax.random.fold_in(key, 17)
    values = jax.random.normal(first_key, shape, jnp.float32)
    return (values * factor).astype(jnp.float32)


def draw_data(key, part):
    shape = (EPOCHS, DATA_ROWS)
    first_key = jax.random.fold_in(key, 23)
    second_key = jax.random.fold_in(key, 29)
    site_scale = jnp.exp(jax.random.uniform(second_key, (1, DATA_ROWS), jnp.float32, 0.0, 2.302585)) / 3.0
    values = jax.random.normal(first_key, shape, jnp.float32)
    return (values * site_scale).astype(jnp.float32)


def setup_inputs(seed: int = 0) -> dict:
    streams_of = jax.random.split(jax.random.key(seed), 5)
    data = draw_data(jax.random.fold_in(streams_of[4], 71), 0)
    blocks = draw_blocks(jax.random.fold_in(streams_of[4], 71), 0)
    block_row = draw_block_row(jax.random.fold_in(streams_of[4], 71), 0)
    block_col = draw_block_col(jax.random.fold_in(streams_of[4], 71), 0)
    return {"data": data, "blocks": blocks, "block_row": block_row, "block_col": block_col}


highest = lax.Precision.HIGHEST
epsilon = 1e-06

def forward_product(grouped, row_ids, col_ids, live_mask, right_vec):
    epochs = right_vec.shape[0]
    right_grid = right_vec.reshape(epochs, UNKNOWNS // BLOCK_EDGE, BLOCK_EDGE)

    def visit(running, members):
        block_piece, rows_here, cols_here, mask_here = members
        picked = jnp.take(right_grid, cols_here, axis=1)
        product = jnp.einsum('gij,egj->egi', block_piece, picked, precision=highest)
        product = product * mask_here[None, :, None]
        return (running.at[:, rows_here, :].add(product), None)
    zero_total = jnp.zeros((epochs, DATA_ROWS // BLOCK_EDGE, BLOCK_EDGE), jnp.float32)
    running, unused = lax.scan(visit, zero_total, (grouped, row_ids, col_ids, live_mask))
    return running.reshape(epochs, DATA_ROWS)

def transposed_product(grouped, row_ids, col_ids, live_mask, left_vec):
    epochs = left_vec.shape[0]
    left_grid = left_vec.reshape(epochs, DATA_ROWS // BLOCK_EDGE, BLOCK_EDGE)

    def visit(running, members):
        block_piece, rows_here, cols_here, mask_here = members
        picked = jnp.take(left_grid, rows_here, axis=1)
        product = jnp.einsum('gij,egi->egj', block_piece, picked, precision=highest)
        product = product * mask_here[None, :, None]
        return (running.at[:, cols_here, :].add(product), None)
    zero_total = jnp.zeros((epochs, UNKNOWNS // BLOCK_EDGE, BLOCK_EDGE), jnp.float32)
    running, unused = lax.scan(visit, zero_total, (grouped, row_ids, col_ids, live_mask))
    return running.reshape(epochs, UNKNOWNS)

def column_norm(values):
    return jnp.sqrt(lax.optimization_barrier(jnp.sum(values * values, axis=1)) + epsilon)

def reference(data, blocks, block_row, block_col):
    run_count = ALL_SLOTS // DEV_SLOTS
    grouped = blocks.reshape(run_count, DEV_SLOTS, BLOCK_EDGE, BLOCK_EDGE)
    is_live = (block_row >= 0) & (block_col >= 0)
    live_mask = is_live.astype(jnp.float32).reshape(run_count, DEV_SLOTS)
    row_ids = jnp.maximum(block_row, 0).astype(jnp.int32).reshape(run_count, DEV_SLOTS)
    col_ids = jnp.maximum(block_col, 0).astype(jnp.int32).reshape(run_count, DEV_SLOTS)
    beta_norm = column_norm(data)
    left_vec = data / beta_norm[:, None]
    right_vec = transposed_product(grouped, row_ids, col_ids, live_mask, left_vec)
    alpha_norm = column_norm(right_vec)
    right_vec = right_vec / alpha_norm[:, None]
    search = right_vec
    solution = jnp.zeros_like(right_vec)
    phibar = beta_norm
    rhobar = alpha_norm
    for iteration in range(ITERATIONS):
        left_vec = forward_product(grouped, row_ids, col_ids, live_mask, right_vec) - alpha_norm[:, None] * left_vec
        beta_norm = column_norm(left_vec)
        left_vec = left_vec / beta_norm[:, None]
        right_vec = transposed_product(grouped, row_ids, col_ids, live_mask, left_vec) - beta_norm[:, None] * right_vec
        alpha_norm = column_norm(right_vec)
        right_vec = right_vec / alpha_norm[:, None]
        rho_value = jnp.sqrt(rhobar * rhobar + beta_norm * beta_norm)
        cosine = rhobar / rho_value
        sine_value = beta_norm / rho_value
        theta_value = sine_value * alpha_norm
        rhobar = -cosine * alpha_norm
        phi_value = cosine * phibar
        phibar = sine_value * phibar
        solution = solution + (phi_value / rho_value)[:, None] * search
        search = right_vec - (theta_value / rho_value)[:, None] * search
    return solution
```

```python
import functools

import jax
import jax.numpy as jnp
from jax import lax
from jax.experimental import pallas as pl
from jax.experimental.pallas import tpu as pltpu
from jax.sharding import PartitionSpec as P

EPOCHS = 64
EDGE = 128
SLOTS = 288
ROW_BLOCKS = 44
COL_BLOCKS = 88
ITERATIONS = 3
EPS = 1e-06

CHAINS = 2
GROUP = EPOCHS // CHAINS
LANE = GROUP // 2
STAGE = 16
UNROLL = 32
PEERS = (1, 3, 2)

T_CHUNK = COL_BLOCKS // 4 * LANE
T_PIECE = T_CHUNK // 4
F_CHUNK = ROW_BLOCKS // 2 * GROUP
F_PIECE = F_CHUNK // 4

MESH = pl.DeviceIdType.MESH

RS1, RS2, AG2, AG1 = 0, 6, 12, 18
CRS, XRS, XAG, CAG = 24, 25, 28, 31
STAT_Y, STAT_Z, STAT_C, STAT_X = 32, 35, 38, 39
END_C, END_X, END_Y, END_Z = 42, 43, 46, 49
STAT, N_SEM = 32, 52


def dot(a, b, dims):
    return lax.dot_general(a, b, (dims, ((), ())), preferred_element_type=jnp.float32)


def diagonal():
    rows = lax.broadcasted_iota(jnp.int32, (GROUP, EDGE), 0)
    lanes = lax.broadcasted_iota(jnp.int32, (GROUP, EDGE), 1)
    return rows == lanes


def pack(squares):
    total = jnp.sum(squares, axis=1, keepdims=True)
    spread = jnp.where(diagonal(), jnp.broadcast_to(total, (GROUP, EDGE)), 0.0)
    return jnp.broadcast_to(jnp.sum(spread, axis=0, keepdims=True), (8, EDGE))


def unpack(tile):
    spread = jnp.where(diagonal(), jnp.broadcast_to(tile[0:1], (GROUP, EDGE)), 0.0)
    return jnp.broadcast_to(jnp.sum(spread, axis=1, keepdims=True), (GROUP, EDGE))


def kernel(
    table, data, blocks, out,
    stage, pairs, sums, wide, tall, left, right, part_t, part_f,
    recv_t1, recv_t2, recv_c, recv_x, stat, stat_in, scal, solved,
    load_sem, send, recv,
):
    row, col = lax.axis_index("row"), lax.axis_index("col")
    me = {"y": row // 4, "z": row % 4, "x": col // 2, "core": col % 2}

    def peer(axis, step):
        at = dict(me)
        at[axis] = (at[axis] + step) % (2 if axis == "core" else 4)
        return (at["y"] * 4 + at["z"], at["x"] * 2 + at["core"])

    def load(step, slot):
        return pltpu.make_async_copy(
            blocks.at[pl.ds(step * STAGE, STAGE)], stage.at[slot], load_sem.at[slot]
        )

    depth = stage.shape[0]
    for slot in range(depth):
        load(slot, slot).start()

    barrier = pltpu.get_barrier_semaphore()
    partners = [(axis, d) for axis in "yzx" for d in PEERS] + [("core", 1)]
    for axis, d in partners:
        pl.semaphore_signal(barrier, inc=1, device_id=peer(axis, d), device_id_type=MESH)

    zero_tile = jnp.zeros((GROUP, EDGE), jnp.float32)
    sums[SLOTS] = zero_tile
    wide_zero = jnp.zeros((GROUP, EDGE), jnp.bfloat16)
    for block in range(ROW_BLOCKS):
        wide[block, GROUP:, EDGE:] = wide_zero

    def take(round_number, unused):
        for slot in range(depth):
            step = round_number * depth + slot
            load(step, slot).wait()

            def split(i, unused):
                value = stage[slot, i]
                high = value.astype(jnp.bfloat16)
                pairs[step * STAGE + i, :EDGE] = high
                low = value - high.astype(jnp.float32)
                pairs[step * STAGE + i, EDGE:] = low.astype(jnp.bfloat16)
                return unused

            lax.fori_loop(0, STAGE, split, 0, unroll=4)

            @pl.when(step + depth < SLOTS // STAGE)
            def _():
                load(step + depth, slot).start()

        return unused

    lax.fori_loop(0, SLOTS // STAGE // depth, take, 0)
    pl.semaphore_wait(barrier, len(partners))

    def chain(g):
        first = g * GROUP

        def copy(src, dst, number, axis, d):
            return pltpu.make_async_remote_copy(
                src_ref=src, dst_ref=dst, send_sem=send.at[g, number], recv_sem=recv.at[g, number],
                device_id=peer(axis, d), device_id_type=MESH,
            )

        def go(copies):
            for c in copies:
                c.start()
            return copies

        def done(copies):
            for c in copies:
                c.wait_recv()
            for c in copies:
                c.wait_send()

        def rows(start, size):
            return pl.ds(pl.multiple_of(start, 8), size)

        def product(perm, vectors, contract, finish):
            def body(q, running):
                for u in range(UNROLL):
                    p = q * UNROLL + u
                    value = dot(vectors[table[perm + 1, p]], pairs[table[perm, p]], contract)
                    keep = table[perm + 2, p].astype(jnp.float32)
                    running = running * keep + finish(value)
                    sums[p] = running
                return running

            lax.fori_loop(0, SLOTS // UNROLL, body, zero_tile)

        def finish_t(v):
            return v[:GROUP] + v[GROUP:]

        def finish_f(v):
            return v[:GROUP, :EDGE] + v[:GROUP, EDGE:] + v[GROUP:, :EDGE]

        def product_t():
            product(0, wide, ((1,), (0,)), finish_t)

            def place(c, unused):
                value = sums[table[6, c]]
                for half in range(2):
                    part_t[g, half, rows(c * LANE, LANE), :] = value[half * LANE : (half + 1) * LANE]
                return unused

            lax.fori_loop(0, COL_BLOCKS, place, 0, unroll=8)

        def product_f():
            product(3, tall, ((1,), (1,)), finish_f)

            def place(c, unused):
                part_f[g, rows(c * GROUP, GROUP), :] = sums[table[7, c]]
                return unused

            lax.fori_loop(0, ROW_BLOCKS, place, 0, unroll=4)

        def split(value):
            high = value.astype(jnp.bfloat16)
            return high, (value - high.astype(jnp.float32)).astype(jnp.bfloat16)

        def widen(value, c):
            high, low = split(value)
            wide[c, :GROUP, :EDGE] = high
            wide[c, :GROUP, EDGE:] = high
            wide[c, GROUP:, :EDGE] = low

        def convert_data():
            def body(c, squares):
                value = data[first : first + GROUP, pl.ds(pl.multiple_of(c * EDGE, EDGE), EDGE)]
                left[g, rows(c * GROUP, GROUP), :] = value
                widen(value, c)
                return squares + value * value

            return lax.fori_loop(0, ROW_BLOCKS, body, zero_tile, unroll=4)

        def convert_left():
            def body(c, squares):
                value = left[g, rows(c * GROUP, GROUP), :]
                widen(value, c)
                return squares + value * value

            return lax.fori_loop(0, ROW_BLOCKS, body, zero_tile, unroll=4)

        def convert_right(k):
            def body(c, squares):
                value = jnp.concatenate(
                    [right[k, g, half, rows(c * LANE, LANE), :] for half in range(2)], axis=0
                )
                high, low = split(value)
                tall[c, :GROUP] = high
                tall[c, GROUP:] = low
                return squares + value * value

            return lax.fori_loop(0, COL_BLOCKS, body, zero_tile, unroll=4)

        def stat_go(which, number, axis):
            steps = (1,) if axis == "core" else PEERS
            return which, number - STAT, go([
                copy(stat.at[g, which], stat_in.at[g, number - STAT + n], number + n, axis, d)
                for n, d in enumerate(steps)
            ])

        def stat_done(sent):
            which, slot, copies = sent
            done(copies)
            total = stat[g, which]
            for n in range(len(copies)):
                total = total + stat_in[g, slot + n]
            return total

        def own_t(half):
            a, b = (me["y"], me["z"]) if half == 0 else (me["z"], me["y"])
            return a, b

        axes = (("y", "z"), ("z", "y"))

        def reduce_t1():
            copies = []
            for half in range(2):
                a, _ = own_t(half)
                for n, d in enumerate(PEERS):
                    q = (a + d) % 4
                    copies.append(copy(
                        part_t.at[g, half, rows(q * T_CHUNK, T_CHUNK)], recv_t1.at[g, half, n],
                        RS1 + 3 * half + n, axes[half][0], d,
                    ))
            return go(copies)

        def reduce_t2(copies):
            done(copies)
            copies = []
            for half in range(2):
                a, b = own_t(half)
                base = a * T_CHUNK
                for i in range(4):
                    here = rows(base + i * T_PIECE, T_PIECE)
                    at = pl.ds(i * T_PIECE, T_PIECE)
                    part_t[g, half, here, :] = (
                        part_t[g, half, here, :] + recv_t1[g, half, 0, at, :]
                        + recv_t1[g, half, 1, at, :] + recv_t1[g, half, 2, at, :]
                    )
                for n, d in enumerate(PEERS):
                    q = (b + d) % 4
                    copies.append(copy(
                        part_t.at[g, half, rows(base + q * T_PIECE, T_PIECE)], recv_t2.at[g, half, n],
                        RS2 + 3 * half + n, axes[half][1], d,
                    ))
            return go(copies)

        def update_right(copies, k):
            done(copies)
            alpha, beta = scal[g, 0], scal[g, 1]
            scal[g, 2] = 1.0 / beta
            scal[g, 3] = beta / alpha
            copies = []
            for half in range(2):
                a, b = own_t(half)
                base = a * T_CHUNK + b * T_PIECE
                for t in range(T_PIECE // 8):
                    here = rows(base + t * 8, 8)
                    at = pl.ds(t * 8, 8)
                    epoch = rows(half * LANE + (b * T_PIECE + t * 8) % LANE, 8)
                    total = (
                        part_t[g, half, here, :] + recv_t2[g, half, 0, at, :]
                        + recv_t2[g, half, 1, at, :] + recv_t2[g, half, 2, at, :]
                    )
                    value = total * scal[g, 2, epoch, :]
                    if k > 0:
                        value = value - scal[g, 3, epoch, :] * right[k - 1, g, half, here, :]
                    right[k, g, half, here, :] = value
                piece = right.at[k, g, half, rows(base, T_PIECE)]
                for n, d in enumerate(PEERS):
                    copies.append(copy(piece, piece, AG2 + 3 * half + n, axes[half][1], d))
            return go(copies)

        def gather_t1(copies, k):
            done(copies)
            copies = []
            for half in range(2):
                a, _ = own_t(half)
                chunk = right.at[k, g, half, rows(a * T_CHUNK, T_CHUNK)]
                for n, d in enumerate(PEERS):
                    copies.append(copy(chunk, chunk, AG1 + 3 * half + n, axes[half][0], d))
            return go(copies)

        def reduce_c():
            other = 1 - me["core"]
            return go([copy(
                part_f.at[g, rows(other * F_CHUNK, F_CHUNK)], recv_c.at[g], CRS, "core", 1
            )])

        f_base = me["core"] * F_CHUNK

        def reduce_x(copies):
            done(copies)
            for i in range(4):
                here = rows(f_base + i * F_PIECE, F_PIECE)
                part_f[g, here, :] = part_f[g, here, :] + recv_c[g, pl.ds(i * F_PIECE, F_PIECE), :]
            return go([
                copy(part_f.at[g, rows(f_base + (me["x"] + d) % 4 * F_PIECE, F_PIECE)],
                     recv_x.at[g, n], XRS + n, "x", d)
                for n, d in enumerate(PEERS)
            ])

        f_own = f_base + me["x"] * F_PIECE

        def update_left(copies):
            done(copies)
            alpha, beta = scal[g, 0], scal[g, 1]
            scal[g, 2] = 1.0 / alpha
            scal[g, 3] = alpha / beta
            scal[g, 4] = zero_tile
            for t in range(F_PIECE // 8):
                here = rows(f_own + t * 8, 8)
                at = pl.ds(t * 8, 8)
                epoch = rows((me["x"] * F_PIECE + t * 8) % GROUP, 8)
                total = (
                    part_f[g, here, :] + recv_x[g, 0, at, :] + recv_x[g, 1, at, :] + recv_x[g, 2, at, :]
                )
                value = total * scal[g, 2, epoch, :] - scal[g, 3, epoch, :] * left[g, here, :]
                left[g, here, :] = value
                scal[g, 4, epoch, :] = scal[g, 4, epoch, :] + value * value

        def gather_x():
            piece = left.at[g, rows(f_own, F_PIECE)]
            return go([copy(piece, piece, XAG + n, "x", d) for n, d in enumerate(PEERS)])

        def gather_c(copies):
            done(copies)
            chunk = left.at[g, rows(f_base, F_CHUNK)]
            return go([copy(chunk, chunk, CAG, "core", 1)])

        def norm(tile):
            return jnp.sqrt(unpack(tile) + EPS)

        phibar = rhobar = None
        weights, thetas = [], []
        for k in range(ITERATIONS):
            stat[g, 0] = pack(convert_data() if k == 0 else convert_left())
            tiles = stat_go(0, STAT_Y, "y")
            product_t()
            moving = reduce_t1()
            stat[g, 1] = stat_done(tiles)
            tiles = stat_go(1, STAT_Z, "z")
            yield
            moving = reduce_t2(moving)
            beta = norm(stat_done(tiles))
            scal[g, 1] = beta
            if k == 0:
                phibar = beta
            else:
                rho = jnp.sqrt(rhobar * rhobar + beta * beta)
                cosine, sine = rhobar / rho, beta / rho
                weights.append(cosine * phibar / rho)
                phibar = sine * phibar
            yield
            moving = update_right(moving, k)
            yield
            moving = gather_t1(moving, k)
            yield
            done(moving)
            stat[g, 0] = pack(convert_right(k))
            tiles = stat_go(0, STAT_C, "core")
            product_f()
            moving = reduce_c()
            stat[g, 1] = stat_done(tiles)
            tiles = stat_go(1, STAT_X, "x")
            yield
            moving = reduce_x(moving)
            alpha = norm(stat_done(tiles))
            scal[g, 0] = alpha
            scal[g, 5 + k] = 1.0 / alpha
            if k == 0:
                rhobar = alpha
            else:
                thetas.append(sine * alpha / rho)
                rhobar = -cosine * alpha
            yield
            update_left(moving)
            if k < ITERATIONS - 1:
                moving = gather_x()
                yield
                moving = gather_c(moving)
                yield
                done(moving)
        stat[g, 0] = pack(scal[g, 4])
        tiles = stat_go(0, END_C, "core")
        for k in range(2):
            scal[g, 8 + k] = weights[k]
            scal[g, 10 + k] = thetas[k]

        def combine(c, unused):
            for half in range(2):
                here = rows(c * LANE, LANE)
                at = pl.ds(half * LANE, LANE)
                search = right[0, g, half, here, :] * scal[g, 5, at, :]
                total = scal[g, 8, at, :] * search
                search = right[1, g, half, here, :] * scal[g, 6, at, :] - scal[g, 10, at, :] * search
                total = total + scal[g, 9, at, :] * search
                search = right[2, g, half, here, :] * scal[g, 7, at, :] - scal[g, 11, at, :] * search
                right[1, g, half, here, :] = total
                right[2, g, half, here, :] = search
            return unused

        lax.fori_loop(0, COL_BLOCKS, combine, 0, unroll=2)
        stat[g, 1] = stat_done(tiles)
        tiles = stat_go(1, END_X, "x")
        yield
        stat[g, 0] = stat_done(tiles)
        tiles = stat_go(0, END_Y, "y")
        yield
        stat[g, 1] = stat_done(tiles)
        tiles = stat_go(1, END_Z, "z")
        yield
        beta = norm(stat_done(tiles))
        rho = jnp.sqrt(rhobar * rhobar + beta * beta)
        scal[g, 8] = (rhobar / rho) * phibar / rho

        def finish(c, unused):
            for half in range(2):
                here = rows(c * LANE, LANE)
                at = pl.ds(half * LANE, LANE)
                value = right[1, g, half, here, :] + scal[g, 8, at, :] * right[2, g, half, here, :]
                start = first + half * LANE
                out[start : start + LANE, pl.ds(pl.multiple_of(c * EDGE, EDGE), EDGE)] = value
            return unused

        lax.fori_loop(0, COL_BLOCKS, finish, 0, unroll=4)

    running = [chain(g) for g in range(CHAINS)]
    while running:
        running = [c for c in running if next(c, "end") != "end"]


def order(target, source, live, targets):
    slot = jnp.arange(SLOTS, dtype=jnp.int32)
    key = jnp.where(live, target, targets)
    place = key * SLOTS + slot
    rank = jnp.sum((place[None, :] < place[:, None]).astype(jnp.int32), axis=1)
    at = (rank[None, :] == slot[:, None]).astype(jnp.int32)
    perm = jnp.sum(at * slot[None, :], axis=1)
    taken = jnp.sum(at * jnp.where(live, source, 0)[None, :], axis=1)
    keys = jnp.sum(at * key[None, :], axis=1)
    before = jnp.concatenate([jnp.full((1,), -1, jnp.int32), keys[:-1]])
    keep = (keys == before).astype(jnp.int32)
    upto = jnp.sum((key[None, :] <= slot[:, None]).astype(jnp.int32), axis=1)
    has = jnp.sum((key[None, :] == slot[:, None]).astype(jnp.int32), axis=1)
    last = jnp.where((has > 0) & (slot < targets), upto - 1, SLOTS)
    return perm, taken, keep, last


def shards(data, blocks, block_row, block_col):
    live = (block_row >= 0) & (block_col >= 0)
    local_row = block_row - lax.axis_index("row") * ROW_BLOCKS
    local_col = block_col - lax.axis_index("col") * COL_BLOCKS
    perm_t, taken_t, keep_t, last_t = order(local_col, local_row, live, COL_BLOCKS)
    perm_f, taken_f, keep_f, last_f = order(local_row, local_col, live, ROW_BLOCKS)
    table = jnp.stack([perm_t, taken_t, keep_t, perm_f, taken_f, keep_f, last_t, last_f])
    vmem = pl.BlockSpec(memory_space=pltpu.VMEM)
    f32, bf16 = jnp.float32, jnp.bfloat16
    return pl.pallas_call(
        kernel,
        out_shape=jax.ShapeDtypeStruct((EPOCHS, COL_BLOCKS * EDGE), f32),
        in_specs=[pl.BlockSpec(memory_space=pltpu.SMEM), vmem, pl.BlockSpec(memory_space=pl.ANY)],
        out_specs=vmem,
        scratch_shapes=[
            pltpu.VMEM((3, STAGE, EDGE, EDGE), f32),
            pltpu.VMEM((SLOTS, 2 * EDGE, EDGE), bf16),
            pltpu.VMEM((SLOTS + 1, GROUP, EDGE), f32),
            pltpu.VMEM((ROW_BLOCKS, 2 * GROUP, 2 * EDGE), bf16),
            pltpu.VMEM((COL_BLOCKS, 2 * GROUP, EDGE), bf16),
            pltpu.VMEM((CHAINS, ROW_BLOCKS * GROUP, EDGE), f32),
            pltpu.VMEM((ITERATIONS, CHAINS, 2, COL_BLOCKS * LANE, EDGE), f32),
            pltpu.VMEM((CHAINS, 2, COL_BLOCKS * LANE, EDGE), f32),
            pltpu.VMEM((CHAINS, ROW_BLOCKS * GROUP, EDGE), f32),
            pltpu.VMEM((CHAINS, 2, 3, T_CHUNK, EDGE), f32),
            pltpu.VMEM((CHAINS, 2, 3, T_PIECE, EDGE), f32),
            pltpu.VMEM((CHAINS, F_CHUNK, EDGE), f32),
            pltpu.VMEM((CHAINS, 3, F_PIECE, EDGE), f32),
            pltpu.VMEM((CHAINS, 2, 8, EDGE), f32),
            pltpu.VMEM((CHAINS, N_SEM - STAT, 8, EDGE), f32),
            pltpu.VMEM((CHAINS, 12, GROUP, EDGE), f32),
            pltpu.VMEM((8, EDGE), f32),
            pltpu.SemaphoreType.DMA((3,)),
            pltpu.SemaphoreType.DMA((CHAINS, N_SEM)),
            pltpu.SemaphoreType.DMA((CHAINS, N_SEM)),
        ],
        compiler_params=pltpu.CompilerParams(
            collective_id=0, has_side_effects=True, vmem_limit_bytes=62 * 2**20
        ),
    )(table, data, blocks)


def solution(mesh):
    placed = (P(None, "row"), P(("row", "col"), None, None), P(("row", "col")), P(("row", "col")))
    return jax.shard_map(
        shards, mesh=mesh, in_specs=placed, out_specs=P(None, "col"), check_vma=False
    )
```

```python
import functools

import jax
import jax.numpy as jnp
from jax import lax
from jax.experimental import pallas as pl
from jax.experimental.pallas import tpu as pltpu
from jax.sharding import PartitionSpec as P

EPOCHS = 64
EDGE = 128
SLOTS = 288
ROW_BLOCKS = 44
COL_BLOCKS = 88
ITERATIONS = 3
EPS = 1e-06

CHAINS = 2
GROUP = EPOCHS // CHAINS
LANE = GROUP // 2
STAGE = 16
UNROLL = 96
PEERS = (1, 3, 2)
ORDER = "0101010100101001010101010101010101010101010110101010101101010101"

T_CHUNK = COL_BLOCKS // 4 * LANE
T_PIECE = T_CHUNK // 4
T_HALF = T_CHUNK // 2
F_CHUNK = ROW_BLOCKS // 2 * GROUP
F_PIECE = F_CHUNK // 4

MESH = pl.DeviceIdType.MESH

RS1, RS2, AG2, AG1 = 0, 12, 18, 24
CRS, XRS, XAG, CAG = 36, 37, 40, 43
STAT_Y, STAT_Z, STAT_C, STAT_X = 44, 47, 50, 51
END_C, END_X, END_Y, END_Z = 54, 55, 58, 61
STAT, N_SEM = 44, 64


def dot(a, b, dims):
    return lax.dot_general(a, b, (dims, ((), ())), preferred_element_type=jnp.float32)


def diagonal():
    rows = lax.broadcasted_iota(jnp.int32, (GROUP, EDGE), 0)
    lanes = lax.broadcasted_iota(jnp.int32, (GROUP, EDGE), 1)
    return rows == lanes


def pack(squares):
    total = jnp.sum(squares, axis=1, keepdims=True)
    spread = jnp.where(diagonal(), jnp.broadcast_to(total, (GROUP, EDGE)), 0.0)
    return jnp.broadcast_to(jnp.sum(spread, axis=0, keepdims=True), (8, EDGE))


def unpack(tile):
    spread = jnp.where(diagonal(), jnp.broadcast_to(tile[0:1], (GROUP, EDGE)), 0.0)
    return jnp.broadcast_to(jnp.sum(spread, axis=1, keepdims=True), (GROUP, EDGE))


def kernel(
    table, data, blocks, out,
    stage, pairs, sums, wide, tall, left, right, part_t, part_f,
    recv_t1, recv_t2, recv_c, recv_x, stat, stat_in, scal, solved,
    load_sem, send, recv,
):
    row, col = lax.axis_index("row"), lax.axis_index("col")
    me = {"y": row // 4, "z": row % 4, "x": col // 2, "core": col % 2}

    def peer(axis, step):
        at = dict(me)
        at[axis] = (at[axis] + step) % (2 if axis == "core" else 4)
        return (at["y"] * 4 + at["z"], at["x"] * 2 + at["core"])

    def load(step, slot):
        return pltpu.make_async_copy(
            blocks.at[pl.ds(step * STAGE, STAGE)], stage.at[slot], load_sem.at[slot]
        )

    depth = stage.shape[0]
    for slot in range(depth):
        load(slot, slot).start()

    barrier = pltpu.get_barrier_semaphore()
    partners = [(axis, d) for axis in "yzx" for d in PEERS] + [("core", 1)]
    for axis, d in partners:
        pl.semaphore_signal(barrier, inc=1, device_id=peer(axis, d), device_id_type=MESH)

    zero_tile = jnp.zeros((GROUP, EDGE), jnp.float32)
    sums[SLOTS] = zero_tile
    wide_zero = jnp.zeros((GROUP, EDGE), jnp.bfloat16)
    for block in range(ROW_BLOCKS):
        wide[block, GROUP:, EDGE:] = wide_zero

    def take(round_number, unused):
        for slot in range(depth):
            step = round_number * depth + slot
            load(step, slot).wait()

            def split(i, unused):
                value = stage[slot, i]
                high = value.astype(jnp.bfloat16)
                pairs[step * STAGE + i, :EDGE] = high
                low = value - high.astype(jnp.float32)
                pairs[step * STAGE + i, EDGE:] = low.astype(jnp.bfloat16)
                return unused

            lax.fori_loop(0, STAGE, split, 0, unroll=4)

            @pl.when(step + depth < SLOTS // STAGE)
            def _():
                load(step + depth, slot).start()

        return unused

    lax.fori_loop(0, SLOTS // STAGE // depth, take, 0)
    pl.semaphore_wait(barrier, len(partners))

    def chain(g):
        first = g * GROUP

        def copy(src, dst, number, axis, d):
            return pltpu.make_async_remote_copy(
                src_ref=src, dst_ref=dst, send_sem=send.at[g, number], recv_sem=recv.at[g, number],
                device_id=peer(axis, d), device_id_type=MESH,
            )

        def go(copies):
            for c in copies:
                c.start()
            return copies

        def done(copies):
            for c in copies:
                c.wait_recv()
            for c in copies:
                c.wait_send()

        def rows(start, size):
            return pl.ds(pl.multiple_of(start, 8), size)

        def product(perm, vectors, contract, finish, twice):
            def body(q, running):
                for u in range(UNROLL):
                    p = q * UNROLL + u
                    x = vectors[table[perm + 1, p]]
                    if twice:
                        x = jnp.concatenate([x, x], axis=0)
                    value = dot(x, pairs[table[perm, p]], contract)
                    keep = table[perm + 2, p].astype(jnp.float32)
                    running = running * keep + finish(value)
                    sums[p] = running
                return running

            lax.fori_loop(0, SLOTS // UNROLL, body, zero_tile)

        def finish_t(v):
            return v[:GROUP] + v[GROUP:]

        def finish_f(v):
            return v[:GROUP, :EDGE] + v[:GROUP, EDGE:] + v[GROUP : 2 * GROUP, :EDGE]

        def product_t():
            product(0, wide, ((1,), (0,)), finish_t, False)

            def place(c, unused):
                value = sums[table[6, c]]
                for half in range(2):
                    part_t[g, half, rows(c * LANE, LANE), :] = value[half * LANE : (half + 1) * LANE]
                return unused

            lax.fori_loop(0, COL_BLOCKS, place, 0, unroll=8)

        def product_f():
            product(3, tall, ((1,), (1,)), finish_f, True)

            def place(c, unused):
                part_f[g, rows(c * GROUP, GROUP), :] = sums[table[7, c]]
                return unused

            lax.fori_loop(0, ROW_BLOCKS, place, 0, unroll=4)

        def split(value):
            high = value.astype(jnp.bfloat16)
            return high, (value - high.astype(jnp.float32)).astype(jnp.bfloat16)

        def widen(value, c):
            high, low = split(value)
            wide[c, :GROUP, :EDGE] = high
            wide[c, :GROUP, EDGE:] = high
            wide[c, GROUP:, :EDGE] = low

        def convert_data():
            def body(c, squares):
                value = data[first : first + GROUP, pl.ds(pl.multiple_of(c * EDGE, EDGE), EDGE)]
                left[g, rows(c * GROUP, GROUP), :] = value
                widen(value, c)
                return squares + value * value

            return lax.fori_loop(0, ROW_BLOCKS, body, zero_tile, unroll=4)

        def convert_left():
            def body(c, squares):
                value = left[g, rows(c * GROUP, GROUP), :]
                widen(value, c)
                return squares + value * value

            return lax.fori_loop(0, ROW_BLOCKS, body, zero_tile, unroll=4)

        def convert_right(k):
            def body(c, squares):
                value = jnp.concatenate(
                    [right[k, g, half, rows(c * LANE, LANE), :] for half in range(2)], axis=0
                )
                high, low = split(value)
                tall[c, :GROUP] = high
                tall[c, GROUP:] = low
                return squares + value * value

            return lax.fori_loop(0, COL_BLOCKS, body, zero_tile, unroll=4)

        def stat_go(which, number, axis):
            steps = (1,) if axis == "core" else PEERS
            return which, number - STAT, go([
                copy(stat.at[g, which], stat_in.at[g, number - STAT + n], number + n, axis, d)
                for n, d in enumerate(steps)
            ])

        def stat_done(sent):
            which, slot, copies = sent
            done(copies)
            total = stat[g, which]
            for n in range(len(copies)):
                total = total + stat_in[g, slot + n]
            return total

        def own_t(half):
            a, b = (me["y"], me["z"]) if half == 0 else (me["z"], me["y"])
            return a, b

        axes = (("y", "z"), ("z", "y"))

        UP, DOWN = 1, 3

        def chunk_rows(ref, half, at, part):
            return ref.at[g, half, rows(at % 4 * T_CHUNK + part * T_HALF, T_HALF)]

        def landing(half, slot, part):
            return recv_t1.at[g, half, slot, pl.ds(part * T_HALF, T_HALF)]

        def reduce_t1():
            far, near = [], []
            for half in range(2):
                a, _ = own_t(half)
                axis, sem = axes[half][0], RS1 + 6 * half
                far += [
                    copy(chunk_rows(part_t, half, a + 2, 0), landing(half, 2, 0), sem, axis, UP),
                    copy(chunk_rows(part_t, half, a + 2, 1), landing(half, 2, 1), sem + 1, axis, DOWN),
                ]
                near += [
                    copy(chunk_rows(part_t, half, a + 1, 1), landing(half, 0, 1), sem + 2, axis, UP),
                    copy(chunk_rows(part_t, half, a + 3, 0), landing(half, 1, 0), sem + 3, axis, DOWN),
                ]
            return go(far), go(near)

        def pass_t1(moving):
            far, near = moving
            done(far)
            last = []
            for half in range(2):
                a, _ = own_t(half)
                axis, sem = axes[half][0], RS1 + 6 * half + 4
                for part, d in ((0, UP), (1, DOWN)):
                    here = rows((a + d) % 4 * T_CHUNK + part * T_HALF, T_HALF)
                    part_t[g, half, here, :] = (
                        part_t[g, half, here, :] + recv_t1[g, half, 2, pl.ds(part * T_HALF, T_HALF), :]
                    )
                    last.append(copy(
                        chunk_rows(part_t, half, a + d, part), landing(half, part, part), sem + part, axis, d
                    ))
            return near + go(last)

        def reduce_t2(copies):
            done(copies)
            copies = []
            for half in range(2):
                a, b = own_t(half)
                base = a * T_CHUNK
                for i in range(4):
                    here = rows(base + i * T_PIECE, T_PIECE)
                    at = pl.ds(i * T_PIECE, T_PIECE)
                    part_t[g, half, here, :] = (
                        part_t[g, half, here, :] + recv_t1[g, half, 0, at, :] + recv_t1[g, half, 1, at, :]
                    )
                for n, d in enumerate(PEERS):
                    q = (b + d) % 4
                    copies.append(copy(
                        part_t.at[g, half, rows(base + q * T_PIECE, T_PIECE)], recv_t2.at[g, half, n],
                        RS2 + 3 * half + n, axes[half][1], d,
                    ))
            return go(copies)

        def update_right(copies, k):
            done(copies)
            alpha, beta = scal[g, 0], scal[g, 1]
            scal[g, 2] = 1.0 / beta
            scal[g, 3] = beta / alpha
            copies = []
            for half in range(2):
                a, b = own_t(half)
                base = a * T_CHUNK + b * T_PIECE
                for t in range(T_PIECE // 8):
                    here = rows(base + t * 8, 8)
                    at = pl.ds(t * 8, 8)
                    epoch = rows(half * LANE + (b * T_PIECE + t * 8) % LANE, 8)
                    total = (
                        part_t[g, half, here, :] + recv_t2[g, half, 0, at, :]
                        + recv_t2[g, half, 1, at, :] + recv_t2[g, half, 2, at, :]
                    )
                    value = total * scal[g, 2, epoch, :]
                    if k > 0:
                        value = value - scal[g, 3, epoch, :] * right[k - 1, g, half, here, :]
                    right[k, g, half, here, :] = value
                piece = right.at[k, g, half, rows(base, T_PIECE)]
                for n, d in enumerate(PEERS):
                    copies.append(copy(piece, piece, AG2 + 3 * half + n, axes[half][1], d))
            return go(copies)

        def gather_t1(copies, k):
            done(copies)
            first_half, second_half = [], []
            for half in range(2):
                a, _ = own_t(half)
                axis, sem = axes[half][0], AG1 + 6 * half
                lower, upper = (chunk_rows(right.at[k], half, a, part) for part in (0, 1))
                first_half += [copy(lower, lower, sem, axis, UP), copy(upper, upper, sem + 1, axis, DOWN)]
                second_half += [copy(upper, upper, sem + 2, axis, UP), copy(lower, lower, sem + 3, axis, DOWN)]
            return go(first_half), go(second_half)

        def pass_g1(moving, k):
            first_half, second_half = moving
            done(first_half)
            last = []
            for half in range(2):
                a, _ = own_t(half)
                axis, sem = axes[half][0], AG1 + 6 * half + 4
                lower, upper = (chunk_rows(right.at[k], half, a + d, part) for d, part in ((3, 0), (1, 1)))
                last += [copy(lower, lower, sem, axis, UP), copy(upper, upper, sem + 1, axis, DOWN)]
            return second_half + go(last)

        def reduce_c():
            other = 1 - me["core"]
            return go([copy(
                part_f.at[g, rows(other * F_CHUNK, F_CHUNK)], recv_c.at[g], CRS, "core", 1
            )])

        f_base = me["core"] * F_CHUNK

        def reduce_x(copies):
            done(copies)
            for i in range(4):
                here = rows(f_base + i * F_PIECE, F_PIECE)
                part_f[g, here, :] = part_f[g, here, :] + recv_c[g, pl.ds(i * F_PIECE, F_PIECE), :]
            return go([
                copy(part_f.at[g, rows(f_base + (me["x"] + d) % 4 * F_PIECE, F_PIECE)],
                     recv_x.at[g, n], XRS + n, "x", d)
                for n, d in enumerate(PEERS)
            ])

        f_own = f_base + me["x"] * F_PIECE

        def update_left(copies):
            done(copies)
            alpha, beta = scal[g, 0], scal[g, 1]
            scal[g, 2] = 1.0 / alpha
            scal[g, 3] = alpha / beta
            scal[g, 4] = zero_tile
            for t in range(F_PIECE // 8):
                here = rows(f_own + t * 8, 8)
                at = pl.ds(t * 8, 8)
                epoch = rows((me["x"] * F_PIECE + t * 8) % GROUP, 8)
                total = (
                    part_f[g, here, :] + recv_x[g, 0, at, :] + recv_x[g, 1, at, :] + recv_x[g, 2, at, :]
                )
                value = total * scal[g, 2, epoch, :] - scal[g, 3, epoch, :] * left[g, here, :]
                left[g, here, :] = value
                scal[g, 4, epoch, :] = scal[g, 4, epoch, :] + value * value

        def gather_x():
            piece = left.at[g, rows(f_own, F_PIECE)]
            return go([copy(piece, piece, XAG + n, "x", d) for n, d in enumerate(PEERS)])

        def gather_c(copies):
            done(copies)
            chunk = left.at[g, rows(f_base, F_CHUNK)]
            return go([copy(chunk, chunk, CAG, "core", 1)])

        def norm(tile):
            return jnp.sqrt(unpack(tile) + EPS)

        phibar = rhobar = None
        weights, thetas = [], []
        for k in range(ITERATIONS):
            stat[g, 0] = pack(convert_data() if k == 0 else convert_left())
            tiles = stat_go(0, STAT_Y, "y")
            product_t()
            moving = reduce_t1()
            stat[g, 1] = stat_done(tiles)
            tiles = stat_go(1, STAT_Z, "z")
            yield
            moving = pass_t1(moving)
            yield
            moving = reduce_t2(moving)
            beta = norm(stat_done(tiles))
            scal[g, 1] = beta
            if k == 0:
                phibar = beta
            else:
                rho = jnp.sqrt(rhobar * rhobar + beta * beta)
                cosine, sine = rhobar / rho, beta / rho
                weights.append(cosine * phibar / rho)
                phibar = sine * phibar
            yield
            moving = update_right(moving, k)
            yield
            moving = gather_t1(moving, k)
            yield
            moving = pass_g1(moving, k)
            yield
            done(moving)
            stat[g, 0] = pack(convert_right(k))
            tiles = stat_go(0, STAT_C, "core")
            product_f()
            moving = reduce_c()
            stat[g, 1] = stat_done(tiles)
            tiles = stat_go(1, STAT_X, "x")
            yield
            moving = reduce_x(moving)
            alpha = norm(stat_done(tiles))
            scal[g, 0] = alpha
            scal[g, 5 + k] = 1.0 / alpha
            if k == 0:
                rhobar = alpha
            else:
                thetas.append(sine * alpha / rho)
                rhobar = -cosine * alpha
            yield
            update_left(moving)
            if k < ITERATIONS - 1:
                moving = gather_x()
                yield
                moving = gather_c(moving)
                yield
                done(moving)
        stat[g, 0] = pack(scal[g, 4])
        tiles = stat_go(0, END_C, "core")
        for k in range(2):
            scal[g, 8 + k] = weights[k]
            scal[g, 10 + k] = thetas[k]

        def combine(c, unused):
            for half in range(2):
                here = rows(c * LANE, LANE)
                at = pl.ds(half * LANE, LANE)
                search = right[0, g, half, here, :] * scal[g, 5, at, :]
                total = scal[g, 8, at, :] * search
                search = right[1, g, half, here, :] * scal[g, 6, at, :] - scal[g, 10, at, :] * search
                total = total + scal[g, 9, at, :] * search
                search = right[2, g, half, here, :] * scal[g, 7, at, :] - scal[g, 11, at, :] * search
                right[1, g, half, here, :] = total
                right[2, g, half, here, :] = search
            return unused

        lax.fori_loop(0, COL_BLOCKS, combine, 0, unroll=2)
        stat[g, 1] = stat_done(tiles)
        tiles = stat_go(1, END_X, "x")
        yield
        stat[g, 0] = stat_done(tiles)
        tiles = stat_go(0, END_Y, "y")
        yield
        stat[g, 1] = stat_done(tiles)
        tiles = stat_go(1, END_Z, "z")
        yield
        beta = norm(stat_done(tiles))
        rho = jnp.sqrt(rhobar * rhobar + beta * beta)
        scal[g, 8] = (rhobar / rho) * phibar / rho

        def finish(c, unused):
            for half in range(2):
                here = rows(c * LANE, LANE)
                at = pl.ds(half * LANE, LANE)
                value = right[1, g, half, here, :] + scal[g, 8, at, :] * right[2, g, half, here, :]
                start = first + half * LANE
                out[start : start + LANE, pl.ds(pl.multiple_of(c * EDGE, EDGE), EDGE)] = value
            return unused

        lax.fori_loop(0, COL_BLOCKS, finish, 0, unroll=4)

    running = [chain(g) for g in range(CHAINS)]
    for g in ORDER:
        next(running[int(g)], None)
    for left_over in running:
        assert next(left_over, "end") == "end"


def order(target, source, live, targets):
    slot = jnp.arange(SLOTS, dtype=jnp.int32)
    key = jnp.where(live, target, targets)
    place = key * SLOTS + slot
    rank = jnp.sum((place[None, :] < place[:, None]).astype(jnp.int32), axis=1)
    at = (rank[None, :] == slot[:, None]).astype(jnp.int32)
    perm = jnp.sum(at * slot[None, :], axis=1)
    taken = jnp.sum(at * jnp.where(live, source, 0)[None, :], axis=1)
    keys = jnp.sum(at * key[None, :], axis=1)
    before = jnp.concatenate([jnp.full((1,), -1, jnp.int32), keys[:-1]])
    keep = (keys == before).astype(jnp.int32)
    upto = jnp.sum((key[None, :] <= slot[:, None]).astype(jnp.int32), axis=1)
    has = jnp.sum((key[None, :] == slot[:, None]).astype(jnp.int32), axis=1)
    last = jnp.where((has > 0) & (slot < targets), upto - 1, SLOTS)
    return perm, taken, keep, last


def shards(data, blocks, block_row, block_col):
    live = (block_row >= 0) & (block_col >= 0)
    local_row = block_row - lax.axis_index("row") * ROW_BLOCKS
    local_col = block_col - lax.axis_index("col") * COL_BLOCKS
    perm_t, taken_t, keep_t, last_t = order(local_col, local_row, live, COL_BLOCKS)
    perm_f, taken_f, keep_f, last_f = order(local_row, local_col, live, ROW_BLOCKS)
    table = jnp.stack([perm_t, taken_t, keep_t, perm_f, taken_f, keep_f, last_t, last_f])
    vmem = pl.BlockSpec(memory_space=pltpu.VMEM)
    f32, bf16 = jnp.float32, jnp.bfloat16
    return pl.pallas_call(
        kernel,
        out_shape=jax.ShapeDtypeStruct((EPOCHS, COL_BLOCKS * EDGE), f32),
        in_specs=[pl.BlockSpec(memory_space=pltpu.SMEM), vmem, pl.BlockSpec(memory_space=pl.ANY)],
        out_specs=vmem,
        scratch_shapes=[
            pltpu.VMEM((3, STAGE, EDGE, EDGE), f32),
            pltpu.VMEM((SLOTS, 2 * EDGE, EDGE), bf16),
            pltpu.VMEM((SLOTS + 1, GROUP, EDGE), f32),
            pltpu.VMEM((ROW_BLOCKS, 2 * GROUP, 2 * EDGE), bf16),
            pltpu.VMEM((COL_BLOCKS, 2 * GROUP, EDGE), bf16),
            pltpu.VMEM((CHAINS, ROW_BLOCKS * GROUP, EDGE), f32),
            pltpu.VMEM((ITERATIONS, CHAINS, 2, COL_BLOCKS * LANE, EDGE), f32),
            pltpu.VMEM((CHAINS, 2, COL_BLOCKS * LANE, EDGE), f32),
            pltpu.VMEM((CHAINS, ROW_BLOCKS * GROUP, EDGE), f32),
            pltpu.VMEM((CHAINS, 2, 3, T_CHUNK, EDGE), f32),
            pltpu.VMEM((CHAINS, 2, 3, T_PIECE, EDGE), f32),
            pltpu.VMEM((CHAINS, F_CHUNK, EDGE), f32),
            pltpu.VMEM((CHAINS, 3, F_PIECE, EDGE), f32),
            pltpu.VMEM((CHAINS, 2, 8, EDGE), f32),
            pltpu.VMEM((CHAINS, N_SEM - STAT, 8, EDGE), f32),
            pltpu.VMEM((CHAINS, 12, GROUP, EDGE), f32),
            pltpu.VMEM((8, EDGE), f32),
            pltpu.SemaphoreType.DMA((3,)),
            pltpu.SemaphoreType.DMA((CHAINS, N_SEM)),
            pltpu.SemaphoreType.DMA((CHAINS, N_SEM)),
        ],
        compiler_params=pltpu.CompilerParams(
            collective_id=0, has_side_effects=True, vmem_limit_bytes=62 * 2**20
        ),
    )(table, data, blocks)


def solution(mesh):
    placed = (P(None, "row"), P(("row", "col"), None, None), P(("row", "col")), P(("row", "col")))
    return jax.shard_map(
        shards, mesh=mesh, in_specs=placed, out_specs=P(None, "col"), check_vma=False
    )
```

```python
import functools

import jax
import jax.numpy as jnp
from jax import lax
from jax.experimental import pallas as pl
from jax.experimental.pallas import tpu as pltpu
from jax.sharding import PartitionSpec as P

EPOCHS = 64
EDGE = 128
SLOTS = 288
ROW_BLOCKS = 44
COL_BLOCKS = 88
ITERATIONS = 3
EPS = 1e-06

CHAINS = 2
GROUP = EPOCHS // CHAINS
LANE = GROUP // 2
STAGE = 16
UNROLL = 72
PEERS = (1, 3, 2)
ORDER = "0010101010101010011010010011010101010101010110010011011010101010101101010101"

T_CHUNK = COL_BLOCKS // 4 * LANE
T_PIECE = T_CHUNK // 4
T_HALF = T_CHUNK // 2
F_CHUNK = ROW_BLOCKS // 2 * GROUP
F_PIECE = F_CHUNK // 4

MESH = pl.DeviceIdType.MESH

RS1, RS2, AG2, AG1 = 0, 12, 18, 24
CRS, XRS, XAG, CAG = 36, 37, 40, 43
STAT_Y, STAT_Z, STAT_C, STAT_X = 44, 47, 50, 51
END_C, END_X, END_Y, END_Z = 54, 55, 58, 61
STAT, N_SEM = 44, 64


def dot(a, b, dims):
    return lax.dot_general(a, b, (dims, ((), ())), preferred_element_type=jnp.float32)


def diagonal():
    rows = lax.broadcasted_iota(jnp.int32, (GROUP, EDGE), 0)
    lanes = lax.broadcasted_iota(jnp.int32, (GROUP, EDGE), 1)
    return rows == lanes


def pack(squares):
    total = jnp.sum(squares, axis=1, keepdims=True)
    spread = jnp.where(diagonal(), jnp.broadcast_to(total, (GROUP, EDGE)), 0.0)
    return jnp.broadcast_to(jnp.sum(spread, axis=0, keepdims=True), (8, EDGE))


def unpack(tile):
    spread = jnp.where(diagonal(), jnp.broadcast_to(tile[0:1], (GROUP, EDGE)), 0.0)
    return jnp.broadcast_to(jnp.sum(spread, axis=1, keepdims=True), (GROUP, EDGE))


def kernel(
    table, data, blocks, out,
    stage, pairs, sums, wide, tall, left, right, part_t, part_f,
    recv_t1, recv_t2, recv_c, recv_x, stat, stat_in, scal, solved,
    load_sem, send, recv,
):
    row, col = lax.axis_index("row"), lax.axis_index("col")
    me = {"y": row // 4, "z": row % 4, "x": col // 2, "core": col % 2}

    def peer(axis, step):
        at = dict(me)
        at[axis] = (at[axis] + step) % (2 if axis == "core" else 4)
        return (at["y"] * 4 + at["z"], at["x"] * 2 + at["core"])

    def load(step, slot):
        return pltpu.make_async_copy(
            blocks.at[pl.ds(step * STAGE, STAGE)], stage.at[slot], load_sem.at[slot]
        )

    depth = stage.shape[0]
    for slot in range(depth):
        load(slot, slot).start()

    barrier = pltpu.get_barrier_semaphore()
    partners = [(axis, d) for axis in "yzx" for d in PEERS] + [("core", 1)]
    for axis, d in partners:
        pl.semaphore_signal(barrier, inc=1, device_id=peer(axis, d), device_id_type=MESH)

    zero_tile = jnp.zeros((GROUP, EDGE), jnp.float32)
    wide_zero = jnp.zeros((GROUP, EDGE), jnp.bfloat16)
    for g in range(CHAINS):
        sums[g, SLOTS] = zero_tile
        for block in range(ROW_BLOCKS):
            wide[g, block, GROUP:, EDGE:] = wide_zero

    def take(round_number, unused):
        for slot in range(depth):
            step = round_number * depth + slot
            load(step, slot).wait()

            def split(i, unused):
                value = stage[slot, i]
                high = value.astype(jnp.bfloat16)
                pairs[step * STAGE + i, :EDGE] = high
                low = value - high.astype(jnp.float32)
                pairs[step * STAGE + i, EDGE:] = low.astype(jnp.bfloat16)
                return unused

            lax.fori_loop(0, STAGE, split, 0, unroll=4)

            @pl.when(step + depth < SLOTS // STAGE)
            def _():
                load(step + depth, slot).start()

        return unused

    lax.fori_loop(0, SLOTS // STAGE // depth, take, 0)
    pl.semaphore_wait(barrier, len(partners))

    def chain(g):
        first = g * GROUP

        def copy(src, dst, number, axis, d):
            return pltpu.make_async_remote_copy(
                src_ref=src, dst_ref=dst, send_sem=send.at[g, number], recv_sem=recv.at[g, number],
                device_id=peer(axis, d), device_id_type=MESH,
            )

        def go(copies):
            for c in copies:
                c.start()
            return copies

        def done(copies):
            for c in copies:
                c.wait_recv()
            for c in copies:
                c.wait_send()

        def rows(start, size):
            return pl.ds(pl.multiple_of(start, 8), size)

        def product(perm, vectors, contract, finish, twice):
            def body(q, running):
                for u in range(UNROLL):
                    p = q * UNROLL + u
                    x = vectors[table[perm + 1, p]]
                    if twice:
                        x = jnp.concatenate([x, x], axis=0)
                    value = dot(x, pairs[table[perm, p]], contract)
                    keep = table[perm + 2, p].astype(jnp.float32)
                    running = running * keep + finish(value)
                    sums[g, p] = running
                return running

            rounds = SLOTS // UNROLL
            running = lax.fori_loop(0, rounds // 2, body, zero_tile)
            yield
            lax.fori_loop(rounds // 2, rounds, body, running)

        def finish_t(v):
            return v[:GROUP] + v[GROUP:]

        def finish_f(v):
            return v[:GROUP, :EDGE] + v[:GROUP, EDGE:] + v[GROUP : 2 * GROUP, :EDGE]

        def product_t():
            yield from product(0, wide.at[g], ((1,), (0,)), finish_t, False)

            def place(c, unused):
                value = sums[g, table[6, c]]
                for half in range(2):
                    part_t[g, half, rows(c * LANE, LANE), :] = value[half * LANE : (half + 1) * LANE]
                return unused

            lax.fori_loop(0, COL_BLOCKS, place, 0, unroll=22)

        def product_f():
            yield from product(3, tall.at[g], ((1,), (1,)), finish_f, True)

            def place(c, unused):
                part_f[g, rows(c * GROUP, GROUP), :] = sums[g, table[7, c]]
                return unused

            lax.fori_loop(0, ROW_BLOCKS, place, 0, unroll=11)

        def split(value):
            high = value.astype(jnp.bfloat16)
            return high, (value - high.astype(jnp.float32)).astype(jnp.bfloat16)

        def widen(value, c):
            high, low = split(value)
            wide[g, c, :GROUP, :EDGE] = high
            wide[g, c, :GROUP, EDGE:] = high
            wide[g, c, GROUP:, :EDGE] = low

        def convert_data():
            def body(c, squares):
                value = data[first : first + GROUP, pl.ds(pl.multiple_of(c * EDGE, EDGE), EDGE)]
                left[g, rows(c * GROUP, GROUP), :] = value
                widen(value, c)
                return squares + value * value

            return lax.fori_loop(0, ROW_BLOCKS, body, zero_tile, unroll=11)

        def convert_left():
            def body(c, squares):
                value = left[g, rows(c * GROUP, GROUP), :]
                widen(value, c)
                return squares + value * value

            return lax.fori_loop(0, ROW_BLOCKS, body, zero_tile, unroll=11)

        def convert_right(k):
            def body(c, squares):
                value = jnp.concatenate(
                    [right[k, g, half, rows(c * LANE, LANE), :] for half in range(2)], axis=0
                )
                high, low = split(value)
                tall[g, c, :GROUP] = high
                tall[g, c, GROUP:] = low
                return squares + value * value

            return lax.fori_loop(0, COL_BLOCKS, body, zero_tile, unroll=11)

        def stat_go(which, number, axis):
            steps = (1,) if axis == "core" else PEERS
            return which, number - STAT, go([
                copy(stat.at[g, which], stat_in.at[g, number - STAT + n], number + n, axis, d)
                for n, d in enumerate(steps)
            ])

        def stat_done(sent):
            which, slot, copies = sent
            done(copies)
            total = stat[g, which]
            for n in range(len(copies)):
                total = total + stat_in[g, slot + n]
            return total

        def own_t(half):
            a, b = (me["y"], me["z"]) if half == 0 else (me["z"], me["y"])
            return a, b

        axes = (("y", "z"), ("z", "y"))

        UP, DOWN = 1, 3

        def chunk_rows(ref, half, at, part):
            return ref.at[g, half, rows(at % 4 * T_CHUNK + part * T_HALF, T_HALF)]

        def landing(half, slot, part):
            return recv_t1.at[g, half, slot, pl.ds(part * T_HALF, T_HALF)]

        def reduce_t1():
            far, near = [], []
            for half in range(2):
                a, _ = own_t(half)
                axis, sem = axes[half][0], RS1 + 6 * half
                far += [
                    copy(chunk_rows(part_t, half, a + 2, 0), landing(half, 2, 0), sem, axis, UP),
                    copy(chunk_rows(part_t, half, a + 2, 1), landing(half, 2, 1), sem + 1, axis, DOWN),
                ]
                near += [
                    copy(chunk_rows(part_t, half, a + 1, 1), landing(half, 0, 1), sem + 2, axis, UP),
                    copy(chunk_rows(part_t, half, a + 3, 0), landing(half, 1, 0), sem + 3, axis, DOWN),
                ]
            return go(far), go(near)

        def pass_t1(moving):
            far, near = moving
            done(far)
            last = []
            for half in range(2):
                a, _ = own_t(half)
                axis, sem = axes[half][0], RS1 + 6 * half + 4
                for part, d in ((0, UP), (1, DOWN)):
                    here = rows((a + d) % 4 * T_CHUNK + part * T_HALF, T_HALF)
                    part_t[g, half, here, :] = (
                        part_t[g, half, here, :] + recv_t1[g, half, 2, pl.ds(part * T_HALF, T_HALF), :]
                    )
                    last.append(copy(
                        chunk_rows(part_t, half, a + d, part), landing(half, part, part), sem + part, axis, d
                    ))
            return near + go(last)

        def reduce_t2(copies):
            done(copies)
            copies = []
            for half in range(2):
                a, b = own_t(half)
                base = a * T_CHUNK
                for i in range(4):
                    here = rows(base + i * T_PIECE, T_PIECE)
                    at = pl.ds(i * T_PIECE, T_PIECE)
                    part_t[g, half, here, :] = (
                        part_t[g, half, here, :] + recv_t1[g, half, 0, at, :] + recv_t1[g, half, 1, at, :]
                    )
                for n, d in enumerate(PEERS):
                    q = (b + d) % 4
                    copies.append(copy(
                        part_t.at[g, half, rows(base + q * T_PIECE, T_PIECE)], recv_t2.at[g, half, n],
                        RS2 + 3 * half + n, axes[half][1], d,
                    ))
            return go(copies)

        def update_right(copies, k):
            done(copies)
            alpha, beta = scal[g, 0], scal[g, 1]
            scal[g, 2] = 1.0 / beta
            scal[g, 3] = beta / alpha
            copies = []
            for half in range(2):
                a, b = own_t(half)
                base = a * T_CHUNK + b * T_PIECE
                for t in range(T_PIECE // 8):
                    here = rows(base + t * 8, 8)
                    at = pl.ds(t * 8, 8)
                    epoch = rows(half * LANE + (b * T_PIECE + t * 8) % LANE, 8)
                    total = (
                        part_t[g, half, here, :] + recv_t2[g, half, 0, at, :]
                        + recv_t2[g, half, 1, at, :] + recv_t2[g, half, 2, at, :]
                    )
                    value = total * scal[g, 2, epoch, :]
                    if k > 0:
                        value = value - scal[g, 3, epoch, :] * right[k - 1, g, half, here, :]
                    right[k, g, half, here, :] = value
                piece = right.at[k, g, half, rows(base, T_PIECE)]
                for n, d in enumerate(PEERS):
                    copies.append(copy(piece, piece, AG2 + 3 * half + n, axes[half][1], d))
            return go(copies)

        def gather_t1(copies, k):
            done(copies)
            first_half, second_half = [], []
            for half in range(2):
                a, _ = own_t(half)
                axis, sem = axes[half][0], AG1 + 6 * half
                lower, upper = (chunk_rows(right.at[k], half, a, part) for part in (0, 1))
                first_half += [copy(lower, lower, sem, axis, UP), copy(upper, upper, sem + 1, axis, DOWN)]
                second_half += [copy(upper, upper, sem + 2, axis, UP), copy(lower, lower, sem + 3, axis, DOWN)]
            return go(first_half), go(second_half)

        def pass_g1(moving, k):
            first_half, second_half = moving
            done(first_half)
            last = []
            for half in range(2):
                a, _ = own_t(half)
                axis, sem = axes[half][0], AG1 + 6 * half + 4
                lower, upper = (chunk_rows(right.at[k], half, a + d, part) for d, part in ((3, 0), (1, 1)))
                last += [copy(lower, lower, sem, axis, UP), copy(upper, upper, sem + 1, axis, DOWN)]
            return second_half + go(last)

        def reduce_c():
            other = 1 - me["core"]
            return go([copy(
                part_f.at[g, rows(other * F_CHUNK, F_CHUNK)], recv_c.at[g], CRS, "core", 1
            )])

        f_base = me["core"] * F_CHUNK

        def reduce_x(copies):
            done(copies)
            for i in range(4):
                here = rows(f_base + i * F_PIECE, F_PIECE)
                part_f[g, here, :] = part_f[g, here, :] + recv_c[g, pl.ds(i * F_PIECE, F_PIECE), :]
            return go([
                copy(part_f.at[g, rows(f_base + (me["x"] + d) % 4 * F_PIECE, F_PIECE)],
                     recv_x.at[g, n], XRS + n, "x", d)
                for n, d in enumerate(PEERS)
            ])

        f_own = f_base + me["x"] * F_PIECE

        def update_left(copies):
            done(copies)
            alpha, beta = scal[g, 0], scal[g, 1]
            scal[g, 2] = 1.0 / alpha
            scal[g, 3] = alpha / beta
            scal[g, 4] = zero_tile
            for t in range(F_PIECE // 8):
                here = rows(f_own + t * 8, 8)
                at = pl.ds(t * 8, 8)
                epoch = rows((me["x"] * F_PIECE + t * 8) % GROUP, 8)
                total = (
                    part_f[g, here, :] + recv_x[g, 0, at, :] + recv_x[g, 1, at, :] + recv_x[g, 2, at, :]
                )
                value = total * scal[g, 2, epoch, :] - scal[g, 3, epoch, :] * left[g, here, :]
                left[g, here, :] = value
                scal[g, 4, epoch, :] = scal[g, 4, epoch, :] + value * value

        def gather_x():
            piece = left.at[g, rows(f_own, F_PIECE)]
            return go([copy(piece, piece, XAG + n, "x", d) for n, d in enumerate(PEERS)])

        def gather_c(copies):
            done(copies)
            chunk = left.at[g, rows(f_base, F_CHUNK)]
            return go([copy(chunk, chunk, CAG, "core", 1)])

        def norm(tile):
            return jnp.sqrt(unpack(tile) + EPS)

        phibar = rhobar = None
        weights, thetas = [], []
        for k in range(ITERATIONS):
            stat[g, 0] = pack(convert_data() if k == 0 else convert_left())
            tiles = stat_go(0, STAT_Y, "y")
            yield from product_t()
            moving = reduce_t1()
            stat[g, 1] = stat_done(tiles)
            tiles = stat_go(1, STAT_Z, "z")
            yield
            moving = pass_t1(moving)
            yield
            moving = reduce_t2(moving)
            beta = norm(stat_done(tiles))
            scal[g, 1] = beta
            if k == 0:
                phibar = beta
            else:
                rho = jnp.sqrt(rhobar * rhobar + beta * beta)
                cosine, sine = rhobar / rho, beta / rho
                weights.append(cosine * phibar / rho)
                phibar = sine * phibar
            yield
            moving = update_right(moving, k)
            yield
            moving = gather_t1(moving, k)
            yield
            moving = pass_g1(moving, k)
            yield
            done(moving)
            stat[g, 0] = pack(convert_right(k))
            tiles = stat_go(0, STAT_C, "core")
            yield from product_f()
            moving = reduce_c()
            stat[g, 1] = stat_done(tiles)
            tiles = stat_go(1, STAT_X, "x")
            yield
            moving = reduce_x(moving)
            alpha = norm(stat_done(tiles))
            scal[g, 0] = alpha
            scal[g, 5 + k] = 1.0 / alpha
            if k == 0:
                rhobar = alpha
            else:
                thetas.append(sine * alpha / rho)
                rhobar = -cosine * alpha
            yield
            update_left(moving)
            if k < ITERATIONS - 1:
                moving = gather_x()
                yield
                moving = gather_c(moving)
                yield
                done(moving)
        stat[g, 0] = pack(scal[g, 4])
        tiles = stat_go(0, END_C, "core")
        for k in range(2):
            scal[g, 8 + k] = weights[k]
            scal[g, 10 + k] = thetas[k]

        def combine(c, unused):
            for half in range(2):
                here = rows(c * LANE, LANE)
                at = pl.ds(half * LANE, LANE)
                search = right[0, g, half, here, :] * scal[g, 5, at, :]
                total = scal[g, 8, at, :] * search
                search = right[1, g, half, here, :] * scal[g, 6, at, :] - scal[g, 10, at, :] * search
                total = total + scal[g, 9, at, :] * search
                search = right[2, g, half, here, :] * scal[g, 7, at, :] - scal[g, 11, at, :] * search
                right[1, g, half, here, :] = total
                right[2, g, half, here, :] = search
            return unused

        lax.fori_loop(0, COL_BLOCKS, combine, 0, unroll=2)
        stat[g, 1] = stat_done(tiles)
        tiles = stat_go(1, END_X, "x")
        yield
        stat[g, 0] = stat_done(tiles)
        tiles = stat_go(0, END_Y, "y")
        yield
        stat[g, 1] = stat_done(tiles)
        tiles = stat_go(1, END_Z, "z")
        yield
        beta = norm(stat_done(tiles))
        rho = jnp.sqrt(rhobar * rhobar + beta * beta)
        scal[g, 8] = (rhobar / rho) * phibar / rho

        def finish(c, unused):
            for half in range(2):
                here = rows(c * LANE, LANE)
                at = pl.ds(half * LANE, LANE)
                value = right[1, g, half, here, :] + scal[g, 8, at, :] * right[2, g, half, here, :]
                start = first + half * LANE
                out[start : start + LANE, pl.ds(pl.multiple_of(c * EDGE, EDGE), EDGE)] = value
            return unused

        lax.fori_loop(0, COL_BLOCKS, finish, 0, unroll=4)

    running = [chain(g) for g in range(CHAINS)]
    for g in ORDER:
        next(running[int(g)], None)
    for left_over in running:
        assert next(left_over, "end") == "end"


def order(target, source, live, targets):
    slot = jnp.arange(SLOTS, dtype=jnp.int32)
    key = jnp.where(live, target, targets)
    place = key * SLOTS + slot
    rank = jnp.sum((place[None, :] < place[:, None]).astype(jnp.int32), axis=1)
    at = (rank[None, :] == slot[:, None]).astype(jnp.int32)
    perm = jnp.sum(at * slot[None, :], axis=1)
    taken = jnp.sum(at * jnp.where(live, source, 0)[None, :], axis=1)
    keys = jnp.sum(at * key[None, :], axis=1)
    before = jnp.concatenate([jnp.full((1,), -1, jnp.int32), keys[:-1]])
    keep = (keys == before).astype(jnp.int32)
    upto = jnp.sum((key[None, :] <= slot[:, None]).astype(jnp.int32), axis=1)
    has = jnp.sum((key[None, :] == slot[:, None]).astype(jnp.int32), axis=1)
    last = jnp.where((has > 0) & (slot < targets), upto - 1, SLOTS)
    return perm, taken, keep, last


def shards(data, blocks, block_row, block_col):
    live = (block_row >= 0) & (block_col >= 0)
    local_row = block_row - lax.axis_index("row") * ROW_BLOCKS
    local_col = block_col - lax.axis_index("col") * COL_BLOCKS
    perm_t, taken_t, keep_t, last_t = order(local_col, local_row, live, COL_BLOCKS)
    perm_f, taken_f, keep_f, last_f = order(local_row, local_col, live, ROW_BLOCKS)
    table = jnp.stack([perm_t, taken_t, keep_t, perm_f, taken_f, keep_f, last_t, last_f])
    vmem = pl.BlockSpec(memory_space=pltpu.VMEM)
    f32, bf16 = jnp.float32, jnp.bfloat16
    return pl.pallas_call(
        kernel,
        out_shape=jax.ShapeDtypeStruct((EPOCHS, COL_BLOCKS * EDGE), f32),
        in_specs=[pl.BlockSpec(memory_space=pltpu.SMEM), vmem, pl.BlockSpec(memory_space=pl.ANY)],
        out_specs=vmem,
        scratch_shapes=[
            pltpu.VMEM((3, STAGE, EDGE, EDGE), f32),
            pltpu.VMEM((SLOTS, 2 * EDGE, EDGE), bf16),
            pltpu.VMEM((CHAINS, SLOTS + 1, GROUP, EDGE), f32),
            pltpu.VMEM((CHAINS, ROW_BLOCKS, 2 * GROUP, 2 * EDGE), bf16),
            pltpu.VMEM((CHAINS, COL_BLOCKS, 2 * GROUP, EDGE), bf16),
            pltpu.VMEM((CHAINS, ROW_BLOCKS * GROUP, EDGE), f32),
            pltpu.VMEM((ITERATIONS, CHAINS, 2, COL_BLOCKS * LANE, EDGE), f32),
            pltpu.VMEM((CHAINS, 2, COL_BLOCKS * LANE, EDGE), f32),
            pltpu.VMEM((CHAINS, ROW_BLOCKS * GROUP, EDGE), f32),
            pltpu.VMEM((CHAINS, 2, 3, T_CHUNK, EDGE), f32),
            pltpu.VMEM((CHAINS, 2, 3, T_PIECE, EDGE), f32),
            pltpu.VMEM((CHAINS, F_CHUNK, EDGE), f32),
            pltpu.VMEM((CHAINS, 3, F_PIECE, EDGE), f32),
            pltpu.VMEM((CHAINS, 2, 8, EDGE), f32),
            pltpu.VMEM((CHAINS, N_SEM - STAT, 8, EDGE), f32),
            pltpu.VMEM((CHAINS, 12, GROUP, EDGE), f32),
            pltpu.VMEM((8, EDGE), f32),
            pltpu.SemaphoreType.DMA((3,)),
            pltpu.SemaphoreType.DMA((CHAINS, N_SEM)),
            pltpu.SemaphoreType.DMA((CHAINS, N_SEM)),
        ],
        compiler_params=pltpu.CompilerParams(
            collective_id=0, has_side_effects=True, vmem_limit_bytes=62 * 2**20
        ),
    )(table, data, blocks)


def solution(mesh):
    placed = (P(None, "row"), P(("row", "col"), None, None), P(("row", "col")), P(("row", "col")))
    return jax.shard_map(
        shards, mesh=mesh, in_specs=placed, out_specs=P(None, "col"), check_vma=False
    )
```

```python
import functools

import jax
import jax.numpy as jnp
from jax import lax
from jax.experimental import pallas as pl
from jax.experimental.pallas import tpu as pltpu
from jax.sharding import PartitionSpec as P

EPOCHS = 64
EDGE = 128
SLOTS = 288
ROW_BLOCKS = 44
COL_BLOCKS = 88
ITERATIONS = 3
EPS = 1e-06

CHAINS = 2
GROUP = EPOCHS // CHAINS
LANE = GROUP // 2
STAGE = 16
UNROLL = 72
PEERS = (1, 3, 2)
ORDER = "00101010101010100110100100110101010101" + "01010110010011011010101010101101010101"

T_CHUNK = COL_BLOCKS // 4 * LANE
T_PIECE = T_CHUNK // 4
T_HALF = T_CHUNK // 2
F_CHUNK = ROW_BLOCKS // 2 * GROUP
F_PIECE = F_CHUNK // 4

MESH = pl.DeviceIdType.MESH

RS1, RS2, AG2, AG1 = 0, 12, 18, 24
CRS, XRS, XAG, CAG = 36, 37, 40, 43
STAT_Y, STAT_Z, STAT_C, STAT_X = 44, 47, 50, 51
END_C, END_X, END_Y, END_Z = 54, 55, 58, 61
STAT, N_SEM = 44, 64


def dot(a, b, dims):
    return lax.dot_general(a, b, (dims, ((), ())), preferred_element_type=jnp.float32)


def diagonal():
    rows = lax.broadcasted_iota(jnp.int32, (GROUP, EDGE), 0)
    lanes = lax.broadcasted_iota(jnp.int32, (GROUP, EDGE), 1)
    return rows == lanes


def pack(squares):
    total = jnp.sum(squares, axis=1, keepdims=True)
    spread = jnp.where(diagonal(), jnp.broadcast_to(total, (GROUP, EDGE)), 0.0)
    return jnp.broadcast_to(jnp.sum(spread, axis=0, keepdims=True), (8, EDGE))


def unpack(tile):
    spread = jnp.where(diagonal(), jnp.broadcast_to(tile[0:1], (GROUP, EDGE)), 0.0)
    return jnp.broadcast_to(jnp.sum(spread, axis=1, keepdims=True), (GROUP, EDGE))


def kernel(
    table, data, blocks, out,
    stage, pairs, sums, wide, tall, left, right, part_t, part_f,
    recv_t1, recv_t2, recv_c, recv_x, stat, stat_in, scal, solved,
    load_sem, send, recv,
):
    row, col = lax.axis_index("row"), lax.axis_index("col")
    me = {"y": row // 4, "z": row % 4, "x": col // 2, "core": col % 2}

    def peer(axis, step):
        at = dict(me)
        at[axis] = (at[axis] + step) % (2 if axis == "core" else 4)
        return (at["y"] * 4 + at["z"], at["x"] * 2 + at["core"])

    def load(step, slot):
        return pltpu.make_async_copy(
            blocks.at[pl.ds(step * STAGE, STAGE)], stage.at[slot], load_sem.at[slot]
        )

    depth = stage.shape[0]
    for slot in range(depth):
        load(slot, slot).start()

    barrier = pltpu.get_barrier_semaphore()
    partners = [(axis, d) for axis in "yzx" for d in PEERS] + [("core", 1)]
    for axis, d in partners:
        pl.semaphore_signal(barrier, inc=1, device_id=peer(axis, d), device_id_type=MESH)

    zero_tile = jnp.zeros((GROUP, EDGE), jnp.float32)
    wide_zero = jnp.zeros((GROUP, EDGE), jnp.bfloat16)
    for g in range(CHAINS):
        sums[g, SLOTS] = zero_tile
        for block in range(ROW_BLOCKS):
            wide[g, block, GROUP:, EDGE:] = wide_zero

    def take(round_number, unused):
        for slot in range(depth):
            step = round_number * depth + slot
            load(step, slot).wait()

            def split(i, unused):
                value = stage[slot, i]
                high = value.astype(jnp.bfloat16)
                pairs[step * STAGE + i, :EDGE] = high
                low = value - high.astype(jnp.float32)
                pairs[step * STAGE + i, EDGE:] = low.astype(jnp.bfloat16)
                return unused

            lax.fori_loop(0, STAGE, split, 0, unroll=4)

            @pl.when(step + depth < SLOTS // STAGE)
            def _():
                load(step + depth, slot).start()

        return unused

    lax.fori_loop(0, SLOTS // STAGE // depth, take, 0)
    pl.semaphore_wait(barrier, len(partners))

    def chain(g):
        first = g * GROUP

        def copy(src, dst, number, axis, d):
            return pltpu.make_async_remote_copy(
                src_ref=src, dst_ref=dst, send_sem=send.at[g, number], recv_sem=recv.at[g, number],
                device_id=peer(axis, d), device_id_type=MESH,
            )

        def go(copies):
            for c in copies:
                c.start()
            return copies

        def done(copies):
            for c in copies:
                c.wait_recv()
            for c in copies:
                c.wait_send()

        def rows(start, size):
            return pl.ds(pl.multiple_of(start, 8), size)

        def product(perm, vectors, contract, finish, twice):
            def body(q, running):
                for u in range(UNROLL):
                    p = q * UNROLL + u
                    x = vectors[table[perm + 1, p]]
                    if twice:
                        x = jnp.concatenate([x, x], axis=0)
                    value = dot(x, pairs[table[perm, p]], contract)
                    keep = table[perm + 2, p].astype(jnp.float32)
                    running = running * keep + finish(value)
                    sums[g, p] = running
                return running

            rounds = SLOTS // UNROLL
            running = lax.fori_loop(0, rounds // 2, body, zero_tile)
            yield
            lax.fori_loop(rounds // 2, rounds, body, running)

        def finish_t(v):
            return v[:GROUP] + v[GROUP:]

        def finish_f(v):
            return v[:GROUP, :EDGE] + v[:GROUP, EDGE:] + v[GROUP : 2 * GROUP, :EDGE]

        def product_t():
            yield from product(0, wide.at[g], ((1,), (0,)), finish_t, False)

            def place(c, unused):
                value = sums[g, table[6, c]]
                for half in range(2):
                    part_t[g, half, rows(c * LANE, LANE), :] = value[half * LANE : (half + 1) * LANE]
                return unused

            lax.fori_loop(0, COL_BLOCKS, place, 0, unroll=22)

        def product_f():
            yield from product(3, tall.at[g], ((1,), (1,)), finish_f, True)

            def place(c, unused):
                part_f[g, rows(c * GROUP, GROUP), :] = sums[g, table[7, c]]
                return unused

            lax.fori_loop(0, ROW_BLOCKS, place, 0, unroll=11)

        def split(value):
            high = value.astype(jnp.bfloat16)
            return high, (value - high.astype(jnp.float32)).astype(jnp.bfloat16)

        def widen(value, c):
            high, low = split(value)
            wide[g, c, :GROUP, :EDGE] = high
            wide[g, c, :GROUP, EDGE:] = high
            wide[g, c, GROUP:, :EDGE] = low

        def convert_data():
            def body(c, squares):
                value = data[first : first + GROUP, pl.ds(pl.multiple_of(c * EDGE, EDGE), EDGE)]
                left[g, rows(c * GROUP, GROUP), :] = value
                widen(value, c)
                return squares + value * value

            return lax.fori_loop(0, ROW_BLOCKS, body, zero_tile, unroll=11)

        def convert_left():
            def body(c, squares):
                value = left[g, rows(c * GROUP, GROUP), :]
                widen(value, c)
                return squares + value * value

            return lax.fori_loop(0, ROW_BLOCKS, body, zero_tile, unroll=11)

        def convert_right(k):
            def body(c, squares):
                value = jnp.concatenate(
                    [right[k, g, half, rows(c * LANE, LANE), :] for half in range(2)], axis=0
                )
                high, low = split(value)
                tall[g, c, :GROUP] = high
                tall[g, c, GROUP:] = low
                return squares + value * value

            return lax.fori_loop(0, COL_BLOCKS, body, zero_tile, unroll=11)

        def stat_go(which, number, axis):
            steps = (1,) if axis == "core" else PEERS
            return which, number - STAT, go([
                copy(stat.at[g, which], stat_in.at[g, number - STAT + n], number + n, axis, d)
                for n, d in enumerate(steps)
            ])

        def stat_done(sent):
            which, slot, copies = sent
            done(copies)
            total = stat[g, which]
            for n in range(len(copies)):
                total = total + stat_in[g, slot + n]
            return total

        def own_t(half):
            a, b = (me["y"], me["z"]) if half == 0 else (me["z"], me["y"])
            return a, b

        axes = (("y", "z"), ("z", "y"))

        UP, DOWN = 1, 3

        def chunk_rows(ref, half, at, part):
            return ref.at[g, half, rows(at % 4 * T_CHUNK + part * T_HALF, T_HALF)]

        def landing(half, slot, part):
            return recv_t1.at[g, half, slot, pl.ds(part * T_HALF, T_HALF)]

        def reduce_t1():
            far, near = [], []
            for half in range(2):
                a, _ = own_t(half)
                axis, sem = axes[half][0], RS1 + 6 * half
                far += [
                    copy(chunk_rows(part_t, half, a + 2, 0), landing(half, 2, 0), sem, axis, UP),
                    copy(chunk_rows(part_t, half, a + 2, 1), landing(half, 2, 1), sem + 1, axis, DOWN),
                ]
                near += [
                    copy(chunk_rows(part_t, half, a + 1, 1), landing(half, 0, 1), sem + 2, axis, UP),
                    copy(chunk_rows(part_t, half, a + 3, 0), landing(half, 1, 0), sem + 3, axis, DOWN),
                ]
            return go(far), go(near)

        def pass_t1(moving):
            far, near = moving
            done(far)
            last = []
            for half in range(2):
                a, _ = own_t(half)
                axis, sem = axes[half][0], RS1 + 6 * half + 4
                for part, d in ((0, UP), (1, DOWN)):
                    here = rows((a + d) % 4 * T_CHUNK + part * T_HALF, T_HALF)
                    part_t[g, half, here, :] = (
                        part_t[g, half, here, :] + recv_t1[g, half, 2, pl.ds(part * T_HALF, T_HALF), :]
                    )
                    last.append(copy(
                        chunk_rows(part_t, half, a + d, part), landing(half, part, part), sem + part, axis, d
                    ))
            return near + go(last)

        def reduce_t2(copies):
            done(copies)
            copies = []
            for half in range(2):
                a, b = own_t(half)
                base = a * T_CHUNK
                for i in range(4):
                    here = rows(base + i * T_PIECE, T_PIECE)
                    at = pl.ds(i * T_PIECE, T_PIECE)
                    part_t[g, half, here, :] = (
                        part_t[g, half, here, :] + recv_t1[g, half, 0, at, :] + recv_t1[g, half, 1, at, :]
                    )
                for n, d in enumerate(PEERS):
                    q = (b + d) % 4
                    copies.append(copy(
                        part_t.at[g, half, rows(base + q * T_PIECE, T_PIECE)], recv_t2.at[g, half, n],
                        RS2 + 3 * half + n, axes[half][1], d,
                    ))
            return go(copies)

        def update_right(copies, k):
            done(copies)
            alpha, beta = scal[g, 0], scal[g, 1]
            scal[g, 2] = 1.0 / beta
            scal[g, 3] = beta / alpha
            copies = []
            for half in range(2):
                a, b = own_t(half)
                base = a * T_CHUNK + b * T_PIECE
                for t in range(T_PIECE // 8):
                    here = rows(base + t * 8, 8)
                    at = pl.ds(t * 8, 8)
                    epoch = rows(half * LANE + (b * T_PIECE + t * 8) % LANE, 8)
                    total = (
                        part_t[g, half, here, :] + recv_t2[g, half, 0, at, :]
                        + recv_t2[g, half, 1, at, :] + recv_t2[g, half, 2, at, :]
                    )
                    value = total * scal[g, 2, epoch, :]
                    if k > 0:
                        value = value - scal[g, 3, epoch, :] * right[k - 1, g, half, here, :]
                    right[k, g, half, here, :] = value
                piece = right.at[k, g, half, rows(base, T_PIECE)]
                for n, d in enumerate(PEERS):
                    copies.append(copy(piece, piece, AG2 + 3 * half + n, axes[half][1], d))
            return go(copies)

        def gather_t1(copies, k):
            done(copies)
            first_half, second_half = [], []
            for half in range(2):
                a, _ = own_t(half)
                axis, sem = axes[half][0], AG1 + 6 * half
                lower, upper = (chunk_rows(right.at[k], half, a, part) for part in (0, 1))
                first_half += [copy(lower, lower, sem, axis, UP), copy(upper, upper, sem + 1, axis, DOWN)]
                second_half += [copy(upper, upper, sem + 2, axis, UP), copy(lower, lower, sem + 3, axis, DOWN)]
            return go(first_half), go(second_half)

        def pass_g1(moving, k):
            first_half, second_half = moving
            done(first_half)
            last = []
            for half in range(2):
                a, _ = own_t(half)
                axis, sem = axes[half][0], AG1 + 6 * half + 4
                lower, upper = (chunk_rows(right.at[k], half, a + d, part) for d, part in ((3, 0), (1, 1)))
                last += [copy(lower, lower, sem, axis, UP), copy(upper, upper, sem + 1, axis, DOWN)]
            return second_half + go(last)

        def reduce_c():
            other = 1 - me["core"]
            return go([copy(
                part_f.at[g, rows(other * F_CHUNK, F_CHUNK)], recv_c.at[g], CRS, "core", 1
            )])

        f_base = me["core"] * F_CHUNK

        def reduce_x(copies):
            done(copies)
            for i in range(4):
                here = rows(f_base + i * F_PIECE, F_PIECE)
                part_f[g, here, :] = part_f[g, here, :] + recv_c[g, pl.ds(i * F_PIECE, F_PIECE), :]
            return go([
                copy(part_f.at[g, rows(f_base + (me["x"] + d) % 4 * F_PIECE, F_PIECE)],
                     recv_x.at[g, n], XRS + n, "x", d)
                for n, d in enumerate(PEERS)
            ])

        f_own = f_base + me["x"] * F_PIECE

        def update_left(copies):
            done(copies)
            alpha, beta = scal[g, 0], scal[g, 1]
            scal[g, 2] = 1.0 / alpha
            scal[g, 3] = alpha / beta
            scal[g, 4] = zero_tile
            for t in range(F_PIECE // 8):
                here = rows(f_own + t * 8, 8)
                at = pl.ds(t * 8, 8)
                epoch = rows((me["x"] * F_PIECE + t * 8) % GROUP, 8)
                total = (
                    part_f[g, here, :] + recv_x[g, 0, at, :] + recv_x[g, 1, at, :] + recv_x[g, 2, at, :]
                )
                value = total * scal[g, 2, epoch, :] - scal[g, 3, epoch, :] * left[g, here, :]
                left[g, here, :] = value
                scal[g, 4, epoch, :] = scal[g, 4, epoch, :] + value * value

        def gather_x():
            piece = left.at[g, rows(f_own, F_PIECE)]
            return go([copy(piece, piece, XAG + n, "x", d) for n, d in enumerate(PEERS)])

        def gather_c(copies):
            done(copies)
            chunk = left.at[g, rows(f_base, F_CHUNK)]
            return go([copy(chunk, chunk, CAG, "core", 1)])

        def norm(tile):
            return jnp.sqrt(unpack(tile) + EPS)

        phibar = rhobar = None
        weights, thetas = [], []
        for k in range(ITERATIONS):
            stat[g, 0] = pack(convert_data() if k == 0 else convert_left())
            tiles = stat_go(0, STAT_Y, "y")
            yield from product_t()
            moving = reduce_t1()
            stat[g, 1] = stat_done(tiles)
            tiles = stat_go(1, STAT_Z, "z")
            yield
            moving = pass_t1(moving)
            yield
            moving = reduce_t2(moving)
            beta = norm(stat_done(tiles))
            scal[g, 1] = beta
            if k == 0:
                phibar = beta
            else:
                rho = jnp.sqrt(rhobar * rhobar + beta * beta)
                cosine, sine = rhobar / rho, beta / rho
                weights.append(cosine * phibar / rho)
                phibar = sine * phibar
            yield
            moving = update_right(moving, k)
            yield
            moving = gather_t1(moving, k)
            yield
            moving = pass_g1(moving, k)
            yield
            done(moving)
            stat[g, 0] = pack(convert_right(k))
            tiles = stat_go(0, STAT_C, "core")
            yield from product_f()
            moving = reduce_c()
            stat[g, 1] = stat_done(tiles)
            tiles = stat_go(1, STAT_X, "x")
            yield
            moving = reduce_x(moving)
            alpha = norm(stat_done(tiles))
            scal[g, 0] = alpha
            scal[g, 5 + k] = 1.0 / alpha
            if k == 0:
                rhobar = alpha
            else:
                thetas.append(sine * alpha / rho)
                rhobar = -cosine * alpha
            yield
            update_left(moving)
            if k < ITERATIONS - 1:
                moving = gather_x()
                yield
                moving = gather_c(moving)
                yield
                done(moving)
        stat[g, 0] = pack(scal[g, 4])
        tiles = stat_go(0, END_C, "core")
        for k in range(2):
            scal[g, 8 + k] = weights[k]
            scal[g, 10 + k] = thetas[k]

        def combine(c, unused):
            for half in range(2):
                here = rows(c * LANE, LANE)
                at = pl.ds(half * LANE, LANE)
                search = right[0, g, half, here, :] * scal[g, 5, at, :]
                total = scal[g, 8, at, :] * search
                search = right[1, g, half, here, :] * scal[g, 6, at, :] - scal[g, 10, at, :] * search
                total = total + scal[g, 9, at, :] * search
                search = right[2, g, half, here, :] * scal[g, 7, at, :] - scal[g, 11, at, :] * search
                right[1, g, half, here, :] = total
                right[2, g, half, here, :] = search
            return unused

        lax.fori_loop(0, COL_BLOCKS, combine, 0, unroll=2)
        stat[g, 1] = stat_done(tiles)
        tiles = stat_go(1, END_X, "x")
        yield
        stat[g, 0] = stat_done(tiles)
        tiles = stat_go(0, END_Y, "y")
        yield
        stat[g, 1] = stat_done(tiles)
        tiles = stat_go(1, END_Z, "z")
        yield
        beta = norm(stat_done(tiles))
        rho = jnp.sqrt(rhobar * rhobar + beta * beta)
        scal[g, 8] = (rhobar / rho) * phibar / rho

        def finish(c, unused):
            for half in range(2):
                here = rows(c * LANE, LANE)
                at = pl.ds(half * LANE, LANE)
                value = right[1, g, half, here, :] + scal[g, 8, at, :] * right[2, g, half, here, :]
                start = first + half * LANE
                out[start : start + LANE, pl.ds(pl.multiple_of(c * EDGE, EDGE), EDGE)] = value
            return unused

        lax.fori_loop(0, COL_BLOCKS, finish, 0, unroll=4)

    running = [chain(g) for g in range(CHAINS)]
    for g in ORDER:
        next(running[int(g)], None)
    for left_over in running:
        assert next(left_over, "end") == "end"


def order(target, source, live, targets):
    slot = jnp.arange(SLOTS, dtype=jnp.int32)
    key = jnp.where(live, target, targets)
    place = key * SLOTS + slot
    rank = jnp.sum((place[None, :] < place[:, None]).astype(jnp.int32), axis=1)
    at = (rank[None, :] == slot[:, None]).astype(jnp.int32)
    perm = jnp.sum(at * slot[None, :], axis=1)
    taken = jnp.sum(at * jnp.where(live, source, 0)[None, :], axis=1)
    keys = jnp.sum(at * key[None, :], axis=1)
    before = jnp.concatenate([jnp.full((1,), -1, jnp.int32), keys[:-1]])
    keep = (keys == before).astype(jnp.int32)
    upto = jnp.sum((key[None, :] <= slot[:, None]).astype(jnp.int32), axis=1)
    has = jnp.sum((key[None, :] == slot[:, None]).astype(jnp.int32), axis=1)
    last = jnp.where((has > 0) & (slot < targets), upto - 1, SLOTS)
    return perm, taken, keep, last


def shards(data, blocks, block_row, block_col):
    live = (block_row >= 0) & (block_col >= 0)
    local_row = block_row - lax.axis_index("row") * ROW_BLOCKS
    local_col = block_col - lax.axis_index("col") * COL_BLOCKS
    perm_t, taken_t, keep_t, last_t = order(local_col, local_row, live, COL_BLOCKS)
    perm_f, taken_f, keep_f, last_f = order(local_row, local_col, live, ROW_BLOCKS)
    table = jnp.stack([perm_t, taken_t, keep_t, perm_f, taken_f, keep_f, last_t, last_f])
    vmem = pl.BlockSpec(memory_space=pltpu.VMEM)
    f32, bf16 = jnp.float32, jnp.bfloat16
    return pl.pallas_call(
        kernel,
        out_shape=jax.ShapeDtypeStruct((EPOCHS, COL_BLOCKS * EDGE), f32),
        in_specs=[pl.BlockSpec(memory_space=pltpu.SMEM), vmem, pl.BlockSpec(memory_space=pl.ANY)],
        out_specs=vmem,
        scratch_shapes=[
            pltpu.VMEM((3, STAGE, EDGE, EDGE), f32),
            pltpu.VMEM((SLOTS, 2 * EDGE, EDGE), bf16),
            pltpu.VMEM((CHAINS, SLOTS + 1, GROUP, EDGE), f32),
            pltpu.VMEM((CHAINS, ROW_BLOCKS, 2 * GROUP, 2 * EDGE), bf16),
            pltpu.VMEM((CHAINS, COL_BLOCKS, 2 * GROUP, EDGE), bf16),
            pltpu.VMEM((CHAINS, ROW_BLOCKS * GROUP, EDGE), f32),
            pltpu.VMEM((ITERATIONS, CHAINS, 2, COL_BLOCKS * LANE, EDGE), f32),
            pltpu.VMEM((CHAINS, 2, COL_BLOCKS * LANE, EDGE), f32),
            pltpu.VMEM((CHAINS, ROW_BLOCKS * GROUP, EDGE), f32),
            pltpu.VMEM((CHAINS, 2, 3, T_CHUNK, EDGE), f32),
            pltpu.VMEM((CHAINS, 2, 3, T_PIECE, EDGE), f32),
            pltpu.VMEM((CHAINS, F_CHUNK, EDGE), f32),
            pltpu.VMEM((CHAINS, 3, F_PIECE, EDGE), f32),
            pltpu.VMEM((CHAINS, 2, 8, EDGE), f32),
            pltpu.VMEM((CHAINS, N_SEM - STAT, 8, EDGE), f32),
            pltpu.VMEM((CHAINS, 12, GROUP, EDGE), f32),
            pltpu.VMEM((8, EDGE), f32),
            pltpu.SemaphoreType.DMA((3,)),
            pltpu.SemaphoreType.DMA((CHAINS, N_SEM)),
            pltpu.SemaphoreType.DMA((CHAINS, N_SEM)),
        ],
        compiler_params=pltpu.CompilerParams(
            collective_id=0, has_side_effects=True, vmem_limit_bytes=62 * 2**20
        ),
    )(table, data, blocks)


def solution(mesh):
    placed = (P(None, "row"), P(("row", "col"), None, None), P(("row", "col")), P(("row", "col")))
    return jax.shard_map(
        shards, mesh=mesh, in_specs=placed, out_specs=P(None, "col"), check_vma=False
    )
```
